32 devices in a mesh: row: 4 (over z), col: 8 (over y, x, core).
Axes of the slice: x: 2, y: 2, z: 4, core: 2. Of those that a mesh axis runs over, the one named last changes fastest.
Arguments:
- embedding: float32 [4096, 256], P(('row', 'col')), may hold values from -6 to 6
- seed_cluster: int32 [4096], P(('row', 'col')), may hold values from 0 to 127
Outputs:
- log_member: float32 [4096, 128], P(('row', 'col'))
The draws below stay inside these ranges and needn't reach their ends.
All inputs are finite; a program needn't handle non-finite values.
Results may differ from the reference program's by a relative error of at most 0.0003.
Values sent between devices are 32-bit elements; how exact they have to be, the bound alone decides.
A program may use at most 64 MiB of HBM per device.

```python
import jax
import jax.numpy as jnp
from jax import lax

FEATURES = 256
CLUSTER_COUNT = 128
POINTS_DEV = 128
SWEEPS = 2
POINTS = 4096
N_COL = 8


def set_ends(result, own_key, smallest, top_value):
    longest = result.shape.index(max(result.shape))
    spots = []
    for shift in (0, 1):
        where = [jax.random.randint(jax.random.fold_in(own_key, axis), (), 0, length) for axis, length in enumerate(result.shape)]
        where[longest] = (where[longest] + shift) % result.shape[longest]
        spots.append(tuple(where))
    return result.at[spots[0]].set(smallest).at[spots[1]].set(top_value)


def block_scale(rng, dims, shards, least, top_value):
    level = 1.0
    for axis_at, parts in shards:
        steps = jax.random.uniform(jax.random.fold_in(jax.random.fold_in(rng, 6), axis_at), (parts,), jnp.float32, least / len(shards), top_value / len(shards))
        level = level * jnp.repeat(jnp.exp(steps), dims[axis_at] // parts).reshape((-1,) + (1,) * (len(dims) - 1 - axis_at))
    return level


def centred(stream_key, shape, spread, limit, shards=(), kind=jnp.bfloat16):
    entries = spread * jax.random.normal(stream_key, shape, jnp.float32)
    if shards:
        entries = entries * block_scale(stream_key, shape, shards, -0.22, 0.18)
    return jnp.clip(entries, -limit, limit).astype(kind)


def setup_inputs(seed: int = 0) -> dict:
    streams_of = jax.random.split(jax.random.key(seed), 3)
    return {
        "embedding": centred(streams_of[0], (POINTS, FEATURES), 1.0, 6.0, ((0, 32),), jnp.float32),
        "seed_cluster": set_ends(jax.random.randint(streams_of[1], (POINTS,), 0, CLUSTER_COUNT), jax.random.fold_in(streams_of[1], 1), 0, CLUSTER_COUNT - 1).astype(jnp.int32),
    }


ANNEAL_TEMP_VALUE = 0.02

def reference(embedding, seed_cluster):
    total = embedding.shape[0]
    squared_norms = lax.optimization_barrier(jnp.sum(embedding * embedding, axis=1))
    cluster_labels = jnp.arange(CLUSTER_COUNT, dtype=jnp.int32)
    member = 0.5 * (seed_cluster[:, None] == cluster_labels[None, :]).astype(jnp.float32) + 0.5 / CLUSTER_COUNT
    height = POINTS_DEV * N_COL
    blocks_x = embedding.reshape(total // height, height, FEATURES)
    blocks_s = squared_norms.reshape(total // height, height)
    log_member = jnp.zeros((total, CLUSTER_COUNT), jnp.float32)
    for sweep in range(SWEEPS):

        def single_block(pair):
            rows, row_sq = pair
            inner = jnp.dot(rows, embedding.T, precision=lax.Precision.HIGHEST)
            distance = jnp.sqrt(row_sq[:, None] + squared_norms[None, :] - 2.0 * inner + 1.0)
            return jnp.dot(distance, member, precision=lax.Precision.HIGHEST)
        attraction = lax.map(single_block, (blocks_x, blocks_s)).reshape(total, CLUSTER_COUNT)
        counts = lax.optimization_barrier(jnp.sum(member, axis=0))
        cohesion = lax.optimization_barrier(jnp.sum(member * attraction, axis=0))
        pair_energy = attraction / counts[None, :] - cohesion[None, :] / (2.0 * counts[None, :] ** 2)
        member_logits = -pair_energy / ANNEAL_TEMP_VALUE
        highest = lax.optimization_barrier(jnp.max(member_logits, axis=1, keepdims=True))
        log_member = member_logits - highest - jnp.log(lax.optimization_barrier(jnp.sum(jnp.exp(member_logits - highest), axis=1, keepdims=True)))
        member = jnp.exp(log_member)
    return log_member
```

```python
import functools

import jax
import jax.numpy as jnp
from jax import lax
from jax.experimental import pallas as pl
from jax.experimental.pallas import tpu as pltpu
from jax.sharding import PartitionSpec as P

CLUSTER_COUNT = 128
SWEEPS = 2
ANNEAL_TEMP_VALUE = 0.02
MESH = pl.DeviceIdType.MESH


def flip(index, offset, size):
    out, bit = 0, 1
    while bit < size:
        out = out + bit * ((index // bit + offset // bit) % 2)
        bit *= 2
    return out


def split3(x):
    first = x.astype(jnp.bfloat16)
    rest = x - first.astype(jnp.float32)
    second = rest.astype(jnp.bfloat16)
    third = (rest - second.astype(jnp.float32)).astype(jnp.bfloat16)
    return first, second, third


def nt(a, b):
    return lax.dot_general(
        a, b, (((1,), (1,)), ((), ())), preferred_element_type=jnp.float32
    )


def nn(a, b):
    return jnp.dot(a, b, preferred_element_type=jnp.float32)


def seeds_to_member(seeds):
    points = seeds.shape[1]
    labels = lax.broadcasted_iota(jnp.int32, (CLUSTER_COUNT, points), 0)
    chosen = jnp.where(labels == seeds, 0.5, 0.0).astype(jnp.float32)
    return chosen.T + 0.5 / CLUSTER_COUNT


def kernel(
    R, C, e_ref, s_ref, o_ref,
    e_row, e_col, s_row, s_col, c1, c2, c3, csq, d1, d2, d3, m1, m2, m3, m_row,
    m_own, m_col, pp, pin, psum, rin, az_own, az_in, ac_own, ac_in,
    er_s, er_r, rel_s, rel_r, ec_s, ec_r, sr_s, sr_r, sc_s, sc_r,
    px_s, px_r, rs_s, rs_r, az_s, az_r, ac_s, ac_r,
    mz_s, mz_r, mc_s, mc_r, mrel_s, mrel_r,
):
    n = e_ref.shape[0]
    Q = C // 2
    r = lax.axis_index("row")
    c = lax.axis_index("col")
    q, b = c // 2, c % 2
    started = []

    def send(src, dst, ssem, rsem, row, col):
        copy = pltpu.make_async_remote_copy(
            src_ref=src, dst_ref=dst, send_sem=ssem, recv_sem=rsem,
            device_id=(row, col), device_id_type=MESH,
        )
        copy.start()
        started.append(copy)
        return copy

    def row_peer(t):
        return flip(r, t, R)

    def chip_peer(s):
        return flip(q, s, Q)

    def col_of(chip, core):
        return chip * 2 + core

    def rows_at(col):
        return pl.ds(pl.multiple_of(col * n, n), n)

    partner = col_of(q, 1 - b)

    barrier = pltpu.get_barrier_semaphore()
    for t in range(1, R):
        pl.semaphore_signal(barrier, inc=1, device_id=(row_peer(t), c), device_id_type=MESH)
    for u in range(1, C):
        pl.semaphore_signal(barrier, inc=1, device_id=(r, flip(c, u, C)), device_id_type=MESH)
    pl.semaphore_wait(barrier, R + C - 2)

    order_q = list(range(Q - 1, 0, -1))
    order_r = list(range(R - 1, 0, -1))
    direct = {}
    for s in order_q:
        direct[s] = send(e_ref, e_row.at[rows_at(c)], er_s.at[s], er_r.at[s], r, col_of(chip_peer(s), b))
    alongz = {}
    for t in order_r:
        alongz[t] = send(e_ref, e_col.at[rows_at(r)], ec_s.at[t], ec_r.at[t], row_peer(t), c)
    direct[0] = send(e_ref, e_row.at[rows_at(c)], er_s.at[0], er_r.at[0], r, partner)
    seeds_col = [None] + [
        send(s_ref, s_row.at[c], sr_s.at[u], sr_r.at[u], r, flip(c, u, C)) for u in range(1, C)
    ]
    seeds_rw = [None] + [
        send(s_ref, s_col.at[r], sc_s.at[t], sc_r.at[t], row_peer(t), c) for t in range(1, R)
    ]

    e_row[rows_at(c), :] = e_ref[...]
    own_member = seeds_to_member(s_ref[...])
    m_row[rows_at(c), :] = own_member

    def ready_column(x, row):
        at = rows_at(row)
        p1, p2, p3 = split3(x)
        c1[at, :] = p1
        c2[at, :] = p2
        c3[at, :] = p3
        q1, q2, q3 = split3(x * x)
        ones = jnp.ones((8, x.shape[1]), jnp.bfloat16)
        csq[:, at] = (nt(ones, q3) + nt(ones, q2)) + nt(ones, q1)

    ready_column(e_ref[...], r)
    m1[rows_at(r), :] = own_member.astype(jnp.bfloat16)

    for u in range(1, C):
        seeds_col[u].wait_recv()
        col = flip(c, u, C)
        m_row[rows_at(col), :] = seeds_to_member(s_row[col])
    for t in range(1, R):
        seeds_rw[t].wait_recv()
        row = row_peer(t)
        m1[rows_at(row), :] = seeds_to_member(s_col[row]).astype(jnp.bfloat16)

    relay = {}

    def forward(s):
        direct[s].wait_recv()
        at = rows_at(col_of(chip_peer(s), b))
        relay[s] = send(e_row.at[at], e_row.at[at], rel_s.at[s], rel_r.at[s], r, partner)

    for i in range(1, max(Q, R)):
        if i < R:
            alongz[i].wait_recv()
            row = row_peer(i)
            ready_column(e_col[rows_at(row), :], row)
        if i < Q:
            forward(i)

    def make_distance(s):
        if s == 0:
            direct[0].wait_recv()
        else:
            relay[s].wait_recv()
        pair = pl.ds(pl.multiple_of(chip_peer(s) * (2 * n), 2 * n), 2 * n)
        x = e_row[pair, :]
        x1, x2, x3 = split3(x)
        inner = nt(x3, c1[...]) + nt(x2, c2[...]) + nt(x1, c3[...])
        inner = inner + (nt(x2, c1[...]) + nt(x1, c2[...]))
        inner = inner + nt(x1, c1[...])
        sq = jnp.sum(x * x, axis=1, keepdims=True)
        distance = jnp.sqrt(sq + csq[0:1, :] - 2.0 * inner + 1.0)
        p1, p2, p3 = split3(distance)
        d1[pair, :] = p1
        d2[pair, :] = p2
        d3[pair, :] = p3
        return (nn(p3, m1[...]) + nn(p2, m1[...])) + nn(p1, m1[...])

    def take_distance(s):
        pair = pl.ds(pl.multiple_of(chip_peer(s) * (2 * n), 2 * n), 2 * n)
        p1, p2, p3 = d1[pair, :], d2[pair, :], d3[pair, :]
        low = nn(p3, m1[...]) + nn(p2, m2[...]) + nn(p1, m3[...])
        mid = nn(p2, m1[...]) + nn(p1, m2[...])
        return low + mid + nn(p1, m1[...])

    log_member = None
    for w in range(SWEEPS):
        order = list(range(Q)) if w == 0 else list(range(Q - 1, -1, -1))
        exchange, scatter = {}, {}

        def combine(s):
            exchange[s].wait_recv()
            psum[w, s] = pp[w, s, b] + pin[w, s]
            if s:
                scatter[s] = send(
                    psum.at[w, s], rin.at[w, s], rs_s.at[w, s], rs_r.at[w, s],
                    r, col_of(chip_peer(s), b),
                )

        cohesion = jnp.zeros((1, CLUSTER_COUNT), jnp.float32)
        if w == 0:
            products = lambda s: make_distance(s)
        else:
            products = lambda s: take_distance(s)
        last = None
        for s in order:
            part = products(s)
            pp[w, s, 0] = part[:n]
            pp[w, s, 1] = part[n:]
            exchange[s] = send(
                pp.at[w, s, 1 - b], pin.at[w, s], px_s.at[w, s], px_r.at[w, s], r, partner
            )
            if w == 0:
                pair = pl.ds(pl.multiple_of(chip_peer(s) * (2 * n), 2 * n), 2 * n)
                cohesion = cohesion + jnp.sum(m_row[pair, :] * part, axis=0, keepdims=True)
            if last is not None:
                combine(last)
            last = s
        if w:
            for s in range(Q):
                (mc[0] if s == 0 else mrel[s]).wait_recv()
            for s in range(Q):
                pair = pl.ds(pl.multiple_of(chip_peer(s) * (2 * n), 2 * n), 2 * n)
                both = jnp.concatenate([pp[w, s, 0], pp[w, s, 1]], axis=0)
                cohesion = cohesion + jnp.sum(m_row[pair, :] * both, axis=0, keepdims=True)

        counts = jnp.sum(own_member, axis=0, keepdims=True)
        az_own[w, 0:1, :] = counts
        az_own[w, 1:2, :] = cohesion
        first = [
            send(az_own.at[w], az_in.at[w, t], az_s.at[w, t], az_r.at[w, t], row_peer(t), c)
            for t in range(1, R)
        ]
        combine(last)
        sums = az_own[w]
        for t in range(1, R):
            first[t - 1].wait_recv()
            sums = sums + az_in[w, t]
        ac_own[w] = sums
        second = [
            send(ac_own.at[w], ac_in.at[w, u], ac_s.at[w, u], ac_r.at[w, u], r, flip(c, u, C))
            for u in range(1, C)
        ]
        attraction = psum[w, 0]
        for s in order:
            if s:
                scatter[s].wait_recv()
                attraction = attraction + rin[w, s]
        for u in range(1, C):
            second[u - 1].wait_recv()
            sums = sums + ac_in[w, u]
        counts, cohesion = sums[0:1, :], sums[1:2, :]
        pair_energy = attraction / counts - cohesion / (2.0 * counts * counts)
        logits = -pair_energy / ANNEAL_TEMP_VALUE
        highest = jnp.max(logits, axis=1, keepdims=True)
        total = jnp.sum(jnp.exp(logits - highest), axis=1, keepdims=True)
        log_member = logits - highest - jnp.log(total)
        if w + 1 < SWEEPS:
            own_member = jnp.exp(log_member)
            m_own[...] = own_member
            mz, mc, mrel = {}, {}, {}
            for t in order_r:
                mz[t] = send(m_own, m_col.at[rows_at(r)], mz_s.at[t], mz_r.at[t], row_peer(t), c)
            for s in order_q:
                mc[s] = send(m_own, m_row.at[rows_at(c)], mc_s.at[s], mc_r.at[s], r, col_of(chip_peer(s), b))
            mc[0] = send(m_own, m_row.at[rows_at(c)], mc_s.at[0], mc_r.at[0], r, partner)
            m_row[rows_at(c), :] = own_member

            def ready_member(x, row):
                at = rows_at(row)
                p1, p2, p3 = split3(x)
                m1[at, :] = p1
                m2[at, :] = p2
                m3[at, :] = p3

            ready_member(own_member, r)
            for i in range(1, max(Q, R)):
                if i < R:
                    mz[i].wait_recv()
                    ready_member(m_col[rows_at(row_peer(i)), :], row_peer(i))
                if i < Q:
                    mc[i].wait_recv()
                    at = rows_at(col_of(chip_peer(i), b))
                    mrel[i] = send(m_row.at[at], m_row.at[at], mrel_s.at[i], mrel_r.at[i], r, partner)

    o_ref[...] = log_member
    for copy in started:
        copy.wait_send()


def shards(R, C, embedding, seed_cluster):
    n, features = embedding.shape
    k = CLUSTER_COUNT
    Q = C // 2
    f32, bf16, i32 = jnp.float32, jnp.bfloat16, jnp.int32
    dma = pltpu.SemaphoreType.DMA
    V = pltpu.VMEM
    return pl.pallas_call(
        functools.partial(kernel, R, C),
        out_shape=jax.ShapeDtypeStruct((n, k), f32),
        in_specs=[pl.BlockSpec(memory_space=pltpu.VMEM)] * 2,
        out_specs=pl.BlockSpec(memory_space=pltpu.VMEM),
        scratch_shapes=[
            V((C * n, features), f32), V((R * n, features), f32),
            V((C, 1, n), i32), V((R, 1, n), i32),
            V((R * n, features), bf16), V((R * n, features), bf16), V((R * n, features), bf16),
            V((8, R * n), f32),
            V((C * n, R * n), bf16), V((C * n, R * n), bf16), V((C * n, R * n), bf16),
            V((R * n, k), bf16), V((R * n, k), bf16), V((R * n, k), bf16),
            V((C * n, k), f32),
            V((n, k), f32), V((R * n, k), f32),
            V((SWEEPS, Q, 2, n, k), f32), V((SWEEPS, Q, n, k), f32),
            V((SWEEPS, Q, n, k), f32), V((SWEEPS, Q, n, k), f32),
            V((SWEEPS, 2, k), f32), V((SWEEPS, R, 2, k), f32),
            V((SWEEPS, 2, k), f32), V((SWEEPS, C, 2, k), f32),
            dma((Q,)), dma((Q,)), dma((Q,)), dma((Q,)), dma((R,)), dma((R,)),
            dma((C,)), dma((C,)), dma((R,)), dma((R,)),
            dma((SWEEPS, Q)), dma((SWEEPS, Q)), dma((SWEEPS, Q)), dma((SWEEPS, Q)),
            dma((SWEEPS, R)), dma((SWEEPS, R)), dma((SWEEPS, C)), dma((SWEEPS, C)),
            dma((R,)), dma((R,)), dma((Q,)), dma((Q,)), dma((Q,)), dma((Q,)),
        ],
        compiler_params=pltpu.CompilerParams(
            collective_id=0, has_side_effects=True, vmem_limit_bytes=60 * 1024 * 1024
        ),
    )(embedding, seed_cluster.reshape(1, n))


def solution(mesh):
    return jax.shard_map(
        functools.partial(shards, mesh.shape["row"], mesh.shape["col"]),
        mesh=mesh,
        in_specs=(P(("row", "col"), None), P(("row", "col"))),
        out_specs=P(("row", "col"), None),
        check_vma=False,
    )
```

```python
import functools

import jax
import jax.numpy as jnp
from jax import lax
from jax.experimental import pallas as pl
from jax.experimental.pallas import tpu as pltpu
from jax.sharding import PartitionSpec as P

CLUSTER_COUNT = 128
SWEEPS = 2
ANNEAL_TEMP_VALUE = 0.02
MESH = pl.DeviceIdType.MESH


def flip(index, offset, size):
    out, bit = 0, 1
    while bit < size:
        out = out + bit * ((index // bit + offset // bit) % 2)
        bit *= 2
    return out


def split3(x):
    first = x.astype(jnp.bfloat16)
    rest = x - first.astype(jnp.float32)
    second = rest.astype(jnp.bfloat16)
    third = (rest - second.astype(jnp.float32)).astype(jnp.bfloat16)
    return first, second, third


def nt(a, b):
    return lax.dot_general(
        a, b, (((1,), (1,)), ((), ())), preferred_element_type=jnp.float32
    )


def nn(a, b):
    return jnp.dot(a, b, preferred_element_type=jnp.float32)


def seeds_to_member(seeds):
    points = seeds.shape[1]
    labels = lax.broadcasted_iota(jnp.int32, (CLUSTER_COUNT, points), 0)
    chosen = jnp.where(labels == seeds, 0.5, 0.0).astype(jnp.float32)
    return chosen.T + 0.5 / CLUSTER_COUNT


def kernel(
    R, C, e_ref, s_ref, o_ref,
    e_row, e_col, s_row, s_col, c1, c2, c3, csq, d1, d2, d3, m1, m2, m3, m_row,
    m_own, m_col, pp, pin, psum, rin, az_own, az_in, ac_own, ac_in, acc,
    er_s, er_r, rel_s, rel_r, ec_s, ec_r, sr_s, sr_r, sc_s, sc_r,
    px_s, px_r, rs_s, rs_r, az_s, az_r, ac_s, ac_r,
    mz_s, mz_r, mc_s, mc_r, mrel_s, mrel_r,
):
    n = e_ref.shape[0]
    Q = C // 2
    r = lax.axis_index("row")
    c = lax.axis_index("col")
    q, b = c // 2, c % 2
    started = []

    def send(src, dst, ssem, rsem, row, col):
        copy = pltpu.make_async_remote_copy(
            src_ref=src, dst_ref=dst, send_sem=ssem, recv_sem=rsem,
            device_id=(row, col), device_id_type=MESH,
        )
        copy.start()
        started.append(copy)
        return copy

    def row_peer(t):
        return flip(r, t, R)

    def chip_peer(s):
        return flip(q, s, Q)

    def col_of(chip, core):
        return chip * 2 + core

    def block(i):
        return pl.ds(i * n, n) if isinstance(i, int) else pl.ds(pl.multiple_of(i * n, n), n)

    def row_slot(s, core):
        return block(2 * s + core)

    def pair_slot(s):
        return pl.ds(2 * s * n, 2 * n)

    partner = col_of(q, 1 - b)
    group = 2 if R % 2 == 0 else 1
    groups = [list(range(g, g + group)) for g in range(0, R, group)]
    near_first = [1] + list(range(R - 1, 1, -1)) if R > 1 else []

    barrier = pltpu.get_barrier_semaphore()
    for t in range(1, R):
        pl.semaphore_signal(barrier, inc=1, device_id=(row_peer(t), c), device_id_type=MESH)
    for u in range(1, C):
        pl.semaphore_signal(barrier, inc=1, device_id=(r, flip(c, u, C)), device_id_type=MESH)

    def ready_column(x, t):
        at = block(t)
        p1, p2, p3 = split3(x)
        c1[at, :] = p1
        c2[at, :] = p2
        c3[at, :] = p3
        q1, q2, q3 = split3(x * x)
        ones = jnp.ones((8, x.shape[1]), jnp.bfloat16)
        csq[:, at] = (nt(ones, q3) + nt(ones, q2)) + nt(ones, q1)

    e_row[row_slot(0, b), :] = e_ref[...]
    own_member = seeds_to_member(s_ref[...])
    m_row[row_slot(0, b), :] = own_member
    m1[block(0), :] = own_member.astype(jnp.bfloat16)
    ready_column(e_ref[...], 0)

    pl.semaphore_wait(barrier, R + C - 2)

    direct, alongz = {}, {}
    for t in near_first:
        alongz[t] = send(e_ref, e_col.at[block(t)], ec_s.at[t], ec_r.at[t], row_peer(t), c)
    for s in range(Q - 1, 0, -1):
        direct[s] = send(
            e_ref, e_row.at[row_slot(s, b)], er_s.at[s], er_r.at[s], r, col_of(chip_peer(s), b)
        )
    direct[0] = send(e_ref, e_row.at[row_slot(0, b)], er_s.at[0], er_r.at[0], r, partner)
    seeds_col = {}
    for s in range(Q):
        for o in range(2):
            if s or o:
                seeds_col[s, o] = send(
                    s_ref, s_row.at[2 * s + b], sr_s.at[2 * s + o], sr_r.at[2 * s + o],
                    r, col_of(chip_peer(s), (b + o) % 2),
                )
    seeds_rw = {}
    for t in range(1, R):
        seeds_rw[t] = send(s_ref, s_col.at[t], sc_s.at[t], sc_r.at[t], row_peer(t), c)

    for s, o in seeds_col:
        seeds_col[s, o].wait_recv()
        core = (b + o) % 2
        m_row[row_slot(s, core), :] = seeds_to_member(s_row[2 * s + core])
    for t in range(1, R):
        seeds_rw[t].wait_recv()
        m1[block(t), :] = seeds_to_member(s_col[t]).astype(jnp.bfloat16)

    relay = {}
    for s in range(1, Q):
        direct[s].wait_recv()
        at = row_slot(s, b)
        relay[s] = send(e_row.at[at], e_row.at[at], rel_s.at[s], rel_r.at[s], r, partner)

    def span(ts):
        return pl.ds(ts[0] * n, len(ts) * n)

    def make_distance(s, ts):
        pair, cols = pair_slot(s), span(ts)
        x = e_row[pair, :]
        x1, x2, x3 = split3(x)
        k1, k2, k3 = c1[cols, :], c2[cols, :], c3[cols, :]
        inner = nt(x3, k1) + nt(x2, k2) + nt(x1, k3)
        inner = inner + (nt(x2, k1) + nt(x1, k2))
        inner = inner + nt(x1, k1)
        sq = jnp.sum(x * x, axis=1, keepdims=True)
        distance = jnp.sqrt(sq + csq[0:1, cols] - 2.0 * inner + 1.0)
        p1, p2, p3 = split3(distance)
        d1[pair, cols] = p1
        d2[pair, cols] = p2
        d3[pair, cols] = p3
        a1 = m1[cols, :]
        return (nn(p3, a1) + nn(p2, a1)) + nn(p1, a1)

    def take_distance(s, ts):
        pair, cols = pair_slot(s), span(ts)
        p1, p2, p3 = d1[pair, cols], d2[pair, cols], d3[pair, cols]
        a1, a2, a3 = m1[cols, :], m2[cols, :], m3[cols, :]
        low = nn(p3, a1) + nn(p2, a2) + nn(p1, a3)
        return low + (nn(p2, a1) + nn(p1, a2)) + nn(p1, a1)

    log_member = None
    mz, mc, mrel = {}, {}, {}
    for w in range(SWEEPS):
        order = list(range(Q - 1, -1, -1))
        exchange, scatter = {}, {}

        def combine(s):
            exchange[s].wait_recv()
            psum[w, s] = pp[w, s, b] + pin[w, s]
            if s:
                scatter[s] = send(
                    psum.at[w, s], rin.at[w, s], rs_s.at[w, s], rs_r.at[w, s],
                    r, col_of(chip_peer(s), b),
                )

        cohesion = jnp.zeros((1, CLUSTER_COUNT), jnp.float32)
        products = make_distance if w == 0 else take_distance
        last = None
        for at, ts in enumerate(groups):
            for t in sorted(ts, reverse=True):
                if t == 0:
                    continue
                if w == 0:
                    alongz[t].wait_recv()
                    ready_column(e_col[block(t), :], t)
                else:
                    mz[t].wait_recv()
                    ready_member(m_col[block(t), :], t)
            final = at + 1 == len(groups)
            for s in (range(Q) if at == 0 else order):
                if at == 0 and w == 0:
                    (direct[0] if s == 0 else relay[s]).wait_recv()
                part = products(s, ts)
                if at:
                    part = part + acc[s]
                if not final:
                    acc[s] = part
                    continue
                pp[w, s, 0] = part[:n]
                pp[w, s, 1] = part[n:]
                exchange[s] = send(
                    pp.at[w, s, 1 - b], pin.at[w, s], px_s.at[w, s], px_r.at[w, s], r, partner
                )
                if w:
                    (mc[0] if s == 0 else mrel[s]).wait_recv()
                cohesion = cohesion + jnp.sum(
                    m_row[pair_slot(s), :] * part, axis=0, keepdims=True
                )
                if last is not None:
                    combine(last)
                last = s
            if w and at == 0:
                for s in range(1, Q):
                    mc[s].wait_recv()
                    slot = row_slot(s, b)
                    mrel[s] = send(m_row.at[slot], m_row.at[slot], mrel_s.at[s], mrel_r.at[s], r, partner)

        counts = jnp.sum(own_member, axis=0, keepdims=True)
        az_own[w, 0:1, :] = counts
        az_own[w, 1:2, :] = cohesion
        first = [
            send(az_own.at[w], az_in.at[w, t], az_s.at[w, t], az_r.at[w, t], row_peer(t), c)
            for t in range(1, R)
        ]
        combine(last)
        sums = az_own[w]
        for t in range(1, R):
            first[t - 1].wait_recv()
            sums = sums + az_in[w, t]
        ac_own[w] = sums
        second = [
            send(ac_own.at[w], ac_in.at[w, u], ac_s.at[w, u], ac_r.at[w, u], r, flip(c, u, C))
            for u in range(1, C)
        ]
        attraction = psum[w, 0]
        for s in order:
            if s:
                scatter[s].wait_recv()
                attraction = attraction + rin[w, s]
        for u in range(1, C):
            second[u - 1].wait_recv()
            sums = sums + ac_in[w, u]
        counts, cohesion = sums[0:1, :], sums[1:2, :]
        pair_energy = attraction / counts - cohesion / (2.0 * counts * counts)
        logits = -pair_energy / ANNEAL_TEMP_VALUE
        highest = jnp.max(logits, axis=1, keepdims=True)
        total = jnp.sum(jnp.exp(logits - highest), axis=1, keepdims=True)
        log_member = logits - highest - jnp.log(total)
        if w + 1 < SWEEPS:
            own_member = jnp.exp(log_member)
            m_own[...] = own_member
            for t in near_first:
                mz[t] = send(m_own, m_col.at[block(t)], mz_s.at[t], mz_r.at[t], row_peer(t), c)
            for s in range(Q - 1, 0, -1):
                mc[s] = send(
                    m_own, m_row.at[row_slot(s, b)], mc_s.at[s], mc_r.at[s], r, col_of(chip_peer(s), b)
                )
            mc[0] = send(m_own, m_row.at[row_slot(0, b)], mc_s.at[0], mc_r.at[0], r, partner)
            m_row[row_slot(0, b), :] = own_member

            def ready_member(x, t):
                at = block(t)
                p1, p2, p3 = split3(x)
                m1[at, :] = p1
                m2[at, :] = p2
                m3[at, :] = p3

            ready_member(own_member, 0)

    o_ref[...] = log_member
    for copy in started:
        copy.wait_send()


def shards(R, C, embedding, seed_cluster):
    n, features = embedding.shape
    k = CLUSTER_COUNT
    Q = C // 2
    f32, bf16, i32 = jnp.float32, jnp.bfloat16, jnp.int32
    dma = pltpu.SemaphoreType.DMA
    V = pltpu.VMEM
    return pl.pallas_call(
        functools.partial(kernel, R, C),
        out_shape=jax.ShapeDtypeStruct((n, k), f32),
        in_specs=[pl.BlockSpec(memory_space=pltpu.VMEM)] * 2,
        out_specs=pl.BlockSpec(memory_space=pltpu.VMEM),
        scratch_shapes=[
            V((C * n, features), f32), V((R * n, features), f32),
            V((C, 1, n), i32), V((R, 1, n), i32),
            V((R * n, features), bf16), V((R * n, features), bf16), V((R * n, features), bf16),
            V((8, R * n), f32),
            V((C * n, R * n), bf16), V((C * n, R * n), bf16), V((C * n, R * n), bf16),
            V((R * n, k), bf16), V((R * n, k), bf16), V((R * n, k), bf16),
            V((C * n, k), f32),
            V((n, k), f32), V((R * n, k), f32),
            V((SWEEPS, Q, 2, n, k), f32), V((SWEEPS, Q, n, k), f32),
            V((SWEEPS, Q, n, k), f32), V((SWEEPS, Q, n, k), f32),
            V((SWEEPS, 2, k), f32), V((SWEEPS, R, 2, k), f32),
            V((SWEEPS, 2, k), f32), V((SWEEPS, C, 2, k), f32),
            V((Q, 2 * n, k), f32),
            dma((Q,)), dma((Q,)), dma((Q,)), dma((Q,)), dma((R,)), dma((R,)),
            dma((C,)), dma((C,)), dma((R,)), dma((R,)),
            dma((SWEEPS, Q)), dma((SWEEPS, Q)), dma((SWEEPS, Q)), dma((SWEEPS, Q)),
            dma((SWEEPS, R)), dma((SWEEPS, R)), dma((SWEEPS, C)), dma((SWEEPS, C)),
            dma((R,)), dma((R,)), dma((Q,)), dma((Q,)), dma((Q,)), dma((Q,)),
        ],
        compiler_params=pltpu.CompilerParams(
            collective_id=0, has_side_effects=True, vmem_limit_bytes=60 * 1024 * 1024
        ),
    )(embedding, seed_cluster.reshape(1, n))


def solution(mesh):
    return jax.shard_map(
        functools.partial(shards, mesh.shape["row"], mesh.shape["col"]),
        mesh=mesh,
        in_specs=(P(("row", "col"), None), P(("row", "col"))),
        out_specs=P(("row", "col"), None),
        check_vma=False,
    )
```

```python
import functools

import jax
import jax.numpy as jnp
from jax import lax
from jax.experimental import pallas as pl
from jax.experimental.pallas import tpu as pltpu
from jax.sharding import PartitionSpec as P

CLUSTER_COUNT = 128
SWEEPS = 2
ANNEAL_TEMP_VALUE = 0.02
MESH = pl.DeviceIdType.MESH


def flip(index, offset, size):
    out, bit = 0, 1
    while bit < size:
        out = out + bit * ((index // bit + offset // bit) % 2)
        bit *= 2
    return out


def split3(x):
    first = x.astype(jnp.bfloat16)
    rest = x - first.astype(jnp.float32)
    second = rest.astype(jnp.bfloat16)
    third = (rest - second.astype(jnp.float32)).astype(jnp.bfloat16)
    return first, second, third


def nt(a, b):
    return lax.dot_general(
        a, b, (((1,), (1,)), ((), ())), preferred_element_type=jnp.float32
    )


def nn(a, b):
    return jnp.dot(a, b, preferred_element_type=jnp.float32)


def seeds_to_member(seeds):
    points = seeds.shape[1]
    labels = lax.broadcasted_iota(jnp.int32, (CLUSTER_COUNT, points), 0)
    chosen = jnp.where(labels == seeds, 0.5, 0.0).astype(jnp.float32)
    return chosen.T + 0.5 / CLUSTER_COUNT


def kernel(
    R, C, e_ref, s_ref, o_ref,
    e_row, e_col, s_row, s_col, c1, c2, c3, csq, d1, d2, d3, m1, m2, m3, m_row,
    m_own, m_col, pp, pin, psum, rin, az_own, az_in, acc,
    er_s, er_r, rel_s, rel_r, ec_s, ec_r, sr_s, sr_r, sc_s, sc_r,
    px_s, px_r, rs_s, rs_r, az_s, az_r,
    mz_s, mz_r, mc_s, mc_r, mrel_s, mrel_r,
):
    n = e_ref.shape[0]
    Q = C // 2
    r = lax.axis_index("row")
    c = lax.axis_index("col")
    q, b = c // 2, c % 2
    started = []

    def send(src, dst, ssem, rsem, row, col):
        copy = pltpu.make_async_remote_copy(
            src_ref=src, dst_ref=dst, send_sem=ssem, recv_sem=rsem,
            device_id=(row, col), device_id_type=MESH,
        )
        copy.start()
        started.append(copy)
        return copy

    def row_peer(t):
        return flip(r, t, R)

    def chip_peer(s):
        return flip(q, s, Q)

    def col_of(chip, core):
        return chip * 2 + core

    def block(i):
        return pl.ds(i * n, n) if isinstance(i, int) else pl.ds(pl.multiple_of(i * n, n), n)

    def row_slot(s, core):
        return block(2 * s + core)

    def pair_slot(s):
        return pl.ds(2 * s * n, 2 * n)

    partner = col_of(q, 1 - b)
    group = 2 if R % 2 == 0 else 1
    groups = [list(range(g, g + group)) for g in range(0, R, group)]
    near_first = [1] + list(range(R - 1, 1, -1)) if R > 1 else []

    barrier = pltpu.get_barrier_semaphore()
    for t in range(1, R):
        pl.semaphore_signal(barrier, inc=1, device_id=(row_peer(t), c), device_id_type=MESH)
    for u in range(1, C):
        pl.semaphore_signal(barrier, inc=1, device_id=(r, flip(c, u, C)), device_id_type=MESH)

    def ready_column(x, t):
        at = block(t)
        p1, p2, p3 = split3(x)
        c1[at, :] = p1
        c2[at, :] = p2
        c3[at, :] = p3
        q1, q2, q3 = split3(x * x)
        ones = jnp.ones((8, x.shape[1]), jnp.bfloat16)
        csq[:, at] = (nt(ones, q3) + nt(ones, q2)) + nt(ones, q1)

    e_row[row_slot(0, b), :] = e_ref[...]
    own_member = seeds_to_member(s_ref[...])
    m_row[row_slot(0, b), :] = own_member
    m1[block(0), :] = own_member.astype(jnp.bfloat16)
    ready_column(e_ref[...], 0)

    pl.semaphore_wait(barrier, R + C - 2)

    seeds_col = {}
    for s in range(Q):
        for o in range(2):
            if s or o:
                seeds_col[s, o] = send(
                    s_ref, s_row.at[2 * s + b], sr_s.at[2 * s + o], sr_r.at[2 * s + o],
                    r, col_of(chip_peer(s), (b + o) % 2),
                )
    seeds_rw = {}
    for t in range(1, R):
        seeds_rw[t] = send(s_ref, s_col.at[t], sc_s.at[t], sc_r.at[t], row_peer(t), c)

    direct, alongz = {}, {}
    for t in near_first:
        alongz[t] = send(e_ref, e_col.at[block(t)], ec_s.at[t], ec_r.at[t], row_peer(t), c)
    for s in range(Q - 1, 0, -1):
        direct[s] = send(
            e_ref, e_row.at[row_slot(s, b)], er_s.at[s], er_r.at[s], r, col_of(chip_peer(s), b)
        )
    direct[0] = send(e_ref, e_row.at[row_slot(0, b)], er_s.at[0], er_r.at[0], r, partner)

    for s, o in seeds_col:
        seeds_col[s, o].wait_recv()
        core = (b + o) % 2
        m_row[row_slot(s, core), :] = seeds_to_member(s_row[2 * s + core])
    for t in range(1, R):
        seeds_rw[t].wait_recv()
        m1[block(t), :] = seeds_to_member(s_col[t]).astype(jnp.bfloat16)

    relay = {}
    for s in range(1, Q):
        direct[s].wait_recv()
        at = row_slot(s, b)
        relay[s] = send(e_row.at[at], e_row.at[at], rel_s.at[s], rel_r.at[s], r, partner)

    def span(ts):
        return pl.ds(ts[0] * n, len(ts) * n)

    def make_distance(s, ts):
        pair, cols = pair_slot(s), span(ts)
        x = e_row[pair, :]
        x1, x2, x3 = split3(x)
        k1, k2, k3 = c1[cols, :], c2[cols, :], c3[cols, :]
        inner = nt(x3, k1) + nt(x2, k2) + nt(x1, k3)
        inner = inner + (nt(x2, k1) + nt(x1, k2))
        inner = inner + nt(x1, k1)
        sq = jnp.sum(x * x, axis=1, keepdims=True)
        distance = jnp.sqrt(sq + csq[0:1, cols] - 2.0 * inner + 1.0)
        p1, p2, p3 = split3(distance)
        d1[pair, cols] = p1
        d2[pair, cols] = p2
        d3[pair, cols] = p3
        a1 = m1[cols, :]
        return (nn(p3, a1) + nn(p2, a1)) + nn(p1, a1)

    def take_distance(s, ts):
        pair, cols = pair_slot(s), span(ts)
        p1, p2, p3 = d1[pair, cols], d2[pair, cols], d3[pair, cols]
        a1, a2, a3 = m1[cols, :], m2[cols, :], m3[cols, :]
        low = nn(p3, a1) + nn(p2, a2) + nn(p1, a3)
        return low + (nn(p2, a1) + nn(p1, a2)) + nn(p1, a1)

    log_member = None
    mz, mc, mrel = {}, {}, {}
    for w in range(SWEEPS):
        order = list(range(Q - 1, -1, -1))
        exchange, scatter = {}, {}

        def combine(s):
            exchange[s].wait_recv()
            psum[w, s] = pp[w, s, b] + pin[w, s]
            if s:
                scatter[s] = send(
                    psum.at[w, s], rin.at[w, s], rs_s.at[w, s], rs_r.at[w, s],
                    r, col_of(chip_peer(s), b),
                )

        cohesion = jnp.zeros((1, CLUSTER_COUNT), jnp.float32)
        products = make_distance if w == 0 else take_distance
        last = None
        for at, ts in enumerate(groups):
            for t in sorted(ts, reverse=True):
                if t == 0:
                    continue
                if w == 0:
                    alongz[t].wait_recv()
                    ready_column(e_col[block(t), :], t)
                else:
                    mz[t].wait_recv()
                    ready_member(m_col[block(t), :], t)
            final = at + 1 == len(groups)
            for s in (range(Q) if at == 0 else order):
                if at == 0 and w == 0:
                    (direct[0] if s == 0 else relay[s]).wait_recv()
                part = products(s, ts)
                if at:
                    part = part + acc[s]
                if not final:
                    acc[s] = part
                    continue
                pp[w, s, 0] = part[:n]
                pp[w, s, 1] = part[n:]
                exchange[s] = send(
                    pp.at[w, s, 1 - b], pin.at[w, s], px_s.at[w, s], px_r.at[w, s], r, partner
                )
                if w:
                    (mc[0] if s == 0 else mrel[s]).wait_recv()
                cohesion = cohesion + jnp.sum(
                    m_row[pair_slot(s), :] * part, axis=0, keepdims=True
                )
                if last is not None:
                    combine(last)
                last = s
            if w and at == 0:
                for s in range(1, Q):
                    mc[s].wait_recv()
                    slot = row_slot(s, b)
                    mrel[s] = send(m_row.at[slot], m_row.at[slot], mrel_s.at[s], mrel_r.at[s], r, partner)

        counts = jnp.sum(own_member, axis=0, keepdims=True)
        az_own[w, 0:1, :] = counts
        az_own[w, 1:2, :] = cohesion
        shares = {}
        for t in range(R - 1, -1, -1):
            for u in range(C - 1, -1, -1):
                if t or u:
                    i = t * C + u
                    shares[i] = send(
                        az_own.at[w], az_in.at[w, i], az_s.at[w, i], az_r.at[w, i],
                        row_peer(t), flip(c, u, C),
                    )
        combine(last)
        attraction = psum[w, 0]
        for s in order:
            if s:
                scatter[s].wait_recv()
                attraction = attraction + rin[w, s]
        for i in shares:
            shares[i].wait_recv()
        az_in[w, 0] = az_own[w]
        sums = jnp.sum(az_in[w], axis=0)
        counts, cohesion = sums[0:1, :], sums[1:2, :]
        pair_energy = attraction / counts - cohesion / (2.0 * counts * counts)
        logits = -pair_energy / ANNEAL_TEMP_VALUE
        highest = jnp.max(logits, axis=1, keepdims=True)
        total = jnp.sum(jnp.exp(logits - highest), axis=1, keepdims=True)
        log_member = logits - highest - jnp.log(total)
        if w + 1 < SWEEPS:
            own_member = jnp.exp(log_member)
            m_own[...] = own_member
            for t in near_first:
                mz[t] = send(m_own, m_col.at[block(t)], mz_s.at[t], mz_r.at[t], row_peer(t), c)
            for s in range(Q - 1, 0, -1):
                mc[s] = send(
                    m_own, m_row.at[row_slot(s, b)], mc_s.at[s], mc_r.at[s], r, col_of(chip_peer(s), b)
                )
            mc[0] = send(m_own, m_row.at[row_slot(0, b)], mc_s.at[0], mc_r.at[0], r, partner)
            m_row[row_slot(0, b), :] = own_member

            def ready_member(x, t):
                at = block(t)
                p1, p2, p3 = split3(x)
                m1[at, :] = p1
                m2[at, :] = p2
                m3[at, :] = p3

            ready_member(own_member, 0)

    o_ref[...] = log_member
    for copy in started:
        copy.wait_send()


def shards(R, C, embedding, seed_cluster):
    n, features = embedding.shape
    k = CLUSTER_COUNT
    Q = C // 2
    f32, bf16, i32 = jnp.float32, jnp.bfloat16, jnp.int32
    dma = pltpu.SemaphoreType.DMA
    V = pltpu.VMEM
    return pl.pallas_call(
        functools.partial(kernel, R, C),
        out_shape=jax.ShapeDtypeStruct((n, k), f32),
        in_specs=[pl.BlockSpec(memory_space=pltpu.VMEM)] * 2,
        out_specs=pl.BlockSpec(memory_space=pltpu.VMEM),
        scratch_shapes=[
            V((C * n, features), f32), V((R * n, features), f32),
            V((C, 1, n), i32), V((R, 1, n), i32),
            V((R * n, features), bf16), V((R * n, features), bf16), V((R * n, features), bf16),
            V((8, R * n), f32),
            V((C * n, R * n), bf16), V((C * n, R * n), bf16), V((C * n, R * n), bf16),
            V((R * n, k), bf16), V((R * n, k), bf16), V((R * n, k), bf16),
            V((C * n, k), f32),
            V((n, k), f32), V((R * n, k), f32),
            V((SWEEPS, Q, 2, n, k), f32), V((SWEEPS, Q, n, k), f32),
            V((SWEEPS, Q, n, k), f32), V((SWEEPS, Q, n, k), f32),
            V((SWEEPS, 2, k), f32), V((SWEEPS, R * C, 2, k), f32),
            V((Q, 2 * n, k), f32),
            dma((Q,)), dma((Q,)), dma((Q,)), dma((Q,)), dma((R,)), dma((R,)),
            dma((C,)), dma((C,)), dma((R,)), dma((R,)),
            dma((SWEEPS, Q)), dma((SWEEPS, Q)), dma((SWEEPS, Q)), dma((SWEEPS, Q)),
            dma((SWEEPS, R * C)), dma((SWEEPS, R * C)),
            dma((R,)), dma((R,)), dma((Q,)), dma((Q,)), dma((Q,)), dma((Q,)),
        ],
        compiler_params=pltpu.CompilerParams(
            collective_id=0, has_side_effects=True, vmem_limit_bytes=60 * 1024 * 1024
        ),
    )(embedding, seed_cluster.reshape(1, n))


def solution(mesh):
    return jax.shard_map(
        functools.partial(shards, mesh.shape["row"], mesh.shape["col"]),
        mesh=mesh,
        in_specs=(P(("row", "col"), None), P(("row", "col"))),
        out_specs=P(("row", "col"), None),
        check_vma=False,
    )
```

```python
import functools

import jax
import jax.numpy as jnp
from jax import lax
from jax.experimental import pallas as pl
from jax.experimental.pallas import tpu as pltpu
from jax.sharding import PartitionSpec as P

CLUSTER_COUNT = 128
SWEEPS = 2
ANNEAL_TEMP_VALUE = 0.02
MESH = pl.DeviceIdType.MESH


def flip(index, offset, size):
    out, bit = 0, 1
    while bit < size:
        out = out + bit * ((index // bit + offset // bit) % 2)
        bit *= 2
    return out


def split3(x):
    first = x.astype(jnp.bfloat16)
    rest = x - first.astype(jnp.float32)
    second = rest.astype(jnp.bfloat16)
    third = (rest - second.astype(jnp.float32)).astype(jnp.bfloat16)
    return first, second, third


def nt(a, b):
    return lax.dot_general(
        a, b, (((1,), (1,)), ((), ())), preferred_element_type=jnp.float32
    )


def nn(a, b):
    return jnp.dot(a, b, preferred_element_type=jnp.float32)


def seeds_to_member(seeds):
    points = seeds.shape[1]
    labels = lax.broadcasted_iota(jnp.int32, (CLUSTER_COUNT, points), 0)
    chosen = jnp.where(labels == seeds, 0.5, 0.0).astype(jnp.float32)
    return chosen.T + 0.5 / CLUSTER_COUNT


def kernel(
    R, C, e_ref, s_ref, o_ref,
    e_row, e_col, s_row, s_col, c1, c2, c3, csq, d1, d2, d3, m1, m2, m3, m_row,
    m_own, m_col, pp, pin, psum, rin, az_own, az_in, acc,
    er_s, er_r, rel_s, rel_r, ec_s, ec_r, sr_s, sr_r, sc_s, sc_r,
    px_s, px_r, rs_s, rs_r, az_s, az_r,
    mz_s, mz_r, mc_s, mc_r, mrel_s, mrel_r,
):
    n = e_ref.shape[0]
    Q = C // 2
    r = lax.axis_index("row")
    c = lax.axis_index("col")
    q, b = c // 2, c % 2
    started = []

    def send(src, dst, ssem, rsem, row, col):
        copy = pltpu.make_async_remote_copy(
            src_ref=src, dst_ref=dst, send_sem=ssem, recv_sem=rsem,
            device_id=(row, col), device_id_type=MESH,
        )
        copy.start()
        started.append(copy)
        return copy

    def row_peer(t):
        return flip(r, t, R)

    def chip_peer(s):
        return flip(q, s, Q)

    def col_of(chip, core):
        return chip * 2 + core

    def block(i):
        return pl.ds(i * n, n) if isinstance(i, int) else pl.ds(pl.multiple_of(i * n, n), n)

    def row_slot(s, core):
        return block(2 * s + core)

    def pair_slot(s):
        return pl.ds(2 * s * n, 2 * n)

    partner = col_of(q, 1 - b)
    group = 2 if R % 2 == 0 else 1
    groups = [list(range(g, g + group)) for g in range(0, R, group)]
    row_order = [t for t in range(2, R)] + [t for t in range(1, min(R, 2))]
    chip_order = list(range(Q - 1, 0, -1))

    def bits(size):
        return [1 << i for i in range(size.bit_length() - 1)]

    barrier = pltpu.get_barrier_semaphore()
    for t in bits(R):
        pl.semaphore_signal(barrier, inc=1, device_id=(row_peer(t), c), device_id_type=MESH)
    for u in bits(C):
        pl.semaphore_signal(barrier, inc=1, device_id=(r, flip(c, u, C)), device_id_type=MESH)

    def ready_column(x, t):
        at = block(t)
        p1, p2, p3 = split3(x)
        c1[at, :] = p1
        c2[at, :] = p2
        c3[at, :] = p3
        q1, q2, q3 = split3(x * x)
        ones = jnp.ones((8, x.shape[1]), jnp.bfloat16)
        csq[:, at] = (nt(ones, q3) + nt(ones, q2)) + nt(ones, q1)

    e_row[row_slot(0, b), :] = e_ref[...]
    own_member = seeds_to_member(s_ref[...])
    m_row[row_slot(0, b), :] = own_member
    m1[block(0), :] = own_member.astype(jnp.bfloat16)
    ready_column(e_ref[...], 0)

    pl.semaphore_wait(barrier, len(bits(R)) + len(bits(C)))

    seeds_col, seeds_rw, direct, alongz = {}, {}, {}, {}

    def send_seeds_col(u):
        seeds_col[u] = send(
            s_ref, s_row.at[(u // 2) * 2 + b], sr_s.at[u], sr_r.at[u], r, flip(c, u, C)
        )

    def send_seeds_rw(t):
        seeds_rw[t] = send(s_ref, s_col.at[t], sc_s.at[t], sc_r.at[t], row_peer(t), c)

    def send_alongz(t):
        alongz[t] = send(e_ref, e_col.at[block(t)], ec_s.at[t], ec_r.at[t], row_peer(t), c)

    def send_direct(s):
        direct[s] = send(
            e_ref, e_row.at[row_slot(s, b)], er_s.at[s], er_r.at[s], r,
            partner if s == 0 else col_of(chip_peer(s), b),
        )

    for t in bits(R):
        send_seeds_rw(t)
    for u in bits(C):
        send_seeds_col(u)
    far_rows, far_chips = bits(R)[::-1], bits(C)[:0:-1]
    for i in range(max(len(far_rows), len(far_chips))):
        if i < len(far_rows):
            send_alongz(far_rows[i])
        if i < len(far_chips):
            send_direct(far_chips[i] // 2)
    send_direct(0)

    heard_row, heard_col = set(), set()
    for t in range(1, R):
        if t not in bits(R):
            via = t - (1 << (t.bit_length() - 1))
            if via not in heard_row:
                seeds_rw[via].wait_recv()
                heard_row.add(via)
            send_seeds_rw(t)
            send_alongz(t)
    for u in range(1, C):
        if u not in bits(C):
            via = u - (1 << (u.bit_length() - 1))
            if via not in heard_col:
                seeds_col[via].wait_recv()
                heard_col.add(via)
            send_seeds_col(u)
            if u % 2 == 0:
                send_direct(u // 2)

    for u in range(1, C):
        if u not in heard_col:
            seeds_col[u].wait_recv()
        core = (b + u) % 2
        m_row[row_slot(u // 2, core), :] = seeds_to_member(s_row[(u // 2) * 2 + core])
    for t in range(1, R):
        if t not in heard_row:
            seeds_rw[t].wait_recv()
        m1[block(t), :] = seeds_to_member(s_col[t]).astype(jnp.bfloat16)

    relay = {}
    for s in range(1, Q):
        direct[s].wait_recv()
        at = row_slot(s, b)
        relay[s] = send(e_row.at[at], e_row.at[at], rel_s.at[s], rel_r.at[s], r, partner)

    def span(ts):
        return pl.ds(ts[0] * n, len(ts) * n)

    def make_distance(s, ts):
        pair, cols = pair_slot(s), span(ts)
        x = e_row[pair, :]
        x1, x2, x3 = split3(x)
        k1, k2, k3 = c1[cols, :], c2[cols, :], c3[cols, :]
        inner = nt(x3, k1) + nt(x2, k2) + nt(x1, k3)
        inner = inner + (nt(x2, k1) + nt(x1, k2))
        inner = inner + nt(x1, k1)
        sq = jnp.sum(x * x, axis=1, keepdims=True)
        distance = jnp.sqrt(sq + csq[0:1, cols] - 2.0 * inner + 1.0)
        p1, p2, p3 = split3(distance)
        d1[pair, cols] = p1
        d2[pair, cols] = p2
        d3[pair, cols] = p3
        a1 = m1[cols, :]
        return (nn(p3, a1) + nn(p2, a1)) + nn(p1, a1)

    def take_distance(s, ts):
        pair, cols = pair_slot(s), span(ts)
        p1, p2, p3 = d1[pair, cols], d2[pair, cols], d3[pair, cols]
        a1, a2, a3 = m1[cols, :], m2[cols, :], m3[cols, :]
        low = nn(p3, a1) + nn(p2, a2) + nn(p1, a3)
        return low + (nn(p2, a1) + nn(p1, a2)) + nn(p1, a1)

    log_member = None
    mz, mc, mrel = {}, {}, {}
    for w in range(SWEEPS):
        order = list(range(Q - 1, -1, -1))
        exchange, scatter = {}, {}

        def combine(s):
            exchange[s].wait_recv()
            psum[w, s] = pp[w, s, b] + pin[w, s]
            if s:
                scatter[s] = send(
                    psum.at[w, s], rin.at[w, s], rs_s.at[w, s], rs_r.at[w, s],
                    r, col_of(chip_peer(s), b),
                )

        cohesion = jnp.zeros((1, CLUSTER_COUNT), jnp.float32)
        products = make_distance if w == 0 else take_distance
        last = None
        for at, ts in enumerate(groups):
            for t in sorted(ts, reverse=True):
                if t == 0:
                    continue
                if w == 0:
                    alongz[t].wait_recv()
                    ready_column(e_col[block(t), :], t)
                else:
                    mz[t].wait_recv()
                    ready_member(m_col[block(t), :], t)
            final = at + 1 == len(groups)
            for s in (range(Q) if at == 0 else order):
                if at == 0 and w == 0:
                    (direct[0] if s == 0 else relay[s]).wait_recv()
                part = products(s, ts)
                if at:
                    part = part + acc[s]
                if not final:
                    acc[s] = part
                    continue
                pp[w, s, 0] = part[:n]
                pp[w, s, 1] = part[n:]
                exchange[s] = send(
                    pp.at[w, s, 1 - b], pin.at[w, s], px_s.at[w, s], px_r.at[w, s], r, partner
                )
                if w:
                    (mc[0] if s == 0 else mrel[s]).wait_recv()
                cohesion = cohesion + jnp.sum(
                    m_row[pair_slot(s), :] * part, axis=0, keepdims=True
                )
                if last is not None:
                    combine(last)
                last = s
            if w and at == 0:
                for s in range(1, Q):
                    mc[s].wait_recv()
                    slot = row_slot(s, b)
                    mrel[s] = send(m_row.at[slot], m_row.at[slot], mrel_s.at[s], mrel_r.at[s], r, partner)

        counts = jnp.sum(own_member, axis=0, keepdims=True)
        az_own[w, 0:1, :] = counts
        az_own[w, 1:2, :] = cohesion
        shares = {}
        for t in range(R - 1, -1, -1):
            for u in range(C - 1, -1, -1):
                if t or u:
                    i = t * C + u
                    shares[i] = send(
                        az_own.at[w], az_in.at[w, i], az_s.at[w, i], az_r.at[w, i],
                        row_peer(t), flip(c, u, C),
                    )
        combine(last)
        attraction = psum[w, 0]
        for s in order:
            if s:
                scatter[s].wait_recv()
                attraction = attraction + rin[w, s]
        for i in shares:
            shares[i].wait_recv()
        az_in[w, 0] = az_own[w]
        sums = jnp.sum(az_in[w], axis=0)
        counts, cohesion = sums[0:1, :], sums[1:2, :]
        pair_energy = attraction / counts - cohesion / (2.0 * counts * counts)
        logits = -pair_energy / ANNEAL_TEMP_VALUE
        highest = jnp.max(logits, axis=1, keepdims=True)
        total = jnp.sum(jnp.exp(logits - highest), axis=1, keepdims=True)
        log_member = logits - highest - jnp.log(total)
        if w + 1 < SWEEPS:
            own_member = jnp.exp(log_member)
            m_own[...] = own_member
            for i in range(max(R, Q) - 1):
                if i < R - 1:
                    t = row_order[i]
                    mz[t] = send(m_own, m_col.at[block(t)], mz_s.at[t], mz_r.at[t], row_peer(t), c)
                if i < Q - 1:
                    s = chip_order[i]
                    mc[s] = send(
                        m_own, m_row.at[row_slot(s, b)], mc_s.at[s], mc_r.at[s],
                        r, col_of(chip_peer(s), b),
                    )
            mc[0] = send(m_own, m_row.at[row_slot(0, b)], mc_s.at[0], mc_r.at[0], r, partner)
            m_row[row_slot(0, b), :] = own_member

            def ready_member(x, t):
                at = block(t)
                p1, p2, p3 = split3(x)
                m1[at, :] = p1
                m2[at, :] = p2
                m3[at, :] = p3

            ready_member(own_member, 0)

    o_ref[...] = log_member
    for copy in started:
        copy.wait_send()


def shards(R, C, embedding, seed_cluster):
    n, features = embedding.shape
    k = CLUSTER_COUNT
    Q = C // 2
    f32, bf16, i32 = jnp.float32, jnp.bfloat16, jnp.int32
    dma = pltpu.SemaphoreType.DMA
    V = pltpu.VMEM
    return pl.pallas_call(
        functools.partial(kernel, R, C),
        out_shape=jax.ShapeDtypeStruct((n, k), f32),
        in_specs=[pl.BlockSpec(memory_space=pltpu.VMEM)] * 2,
        out_specs=pl.BlockSpec(memory_space=pltpu.VMEM),
        scratch_shapes=[
            V((C * n, features), f32), V((R * n, features), f32),
            V((C, 1, n), i32), V((R, 1, n), i32),
            V((R * n, features), bf16), V((R * n, features), bf16), V((R * n, features), bf16),
            V((8, R * n), f32),
            V((C * n, R * n), bf16), V((C * n, R * n), bf16), V((C * n, R * n), bf16),
            V((R * n, k), bf16), V((R * n, k), bf16), V((R * n, k), bf16),
            V((C * n, k), f32),
            V((n, k), f32), V((R * n, k), f32),
            V((SWEEPS, Q, 2, n, k), f32), V((SWEEPS, Q, n, k), f32),
            V((SWEEPS, Q, n, k), f32), V((SWEEPS, Q, n, k), f32),
            V((SWEEPS, 2, k), f32), V((SWEEPS, R * C, 2, k), f32),
            V((Q, 2 * n, k), f32),
            dma((Q,)), dma((Q,)), dma((Q,)), dma((Q,)), dma((R,)), dma((R,)),
            dma((C,)), dma((C,)), dma((R,)), dma((R,)),
            dma((SWEEPS, Q)), dma((SWEEPS, Q)), dma((SWEEPS, Q)), dma((SWEEPS, Q)),
            dma((SWEEPS, R * C)), dma((SWEEPS, R * C)),
            dma((R,)), dma((R,)), dma((Q,)), dma((Q,)), dma((Q,)), dma((Q,)),
        ],
        compiler_params=pltpu.CompilerParams(
            collective_id=0, has_side_effects=True, vmem_limit_bytes=60 * 1024 * 1024
        ),
    )(embedding, seed_cluster.reshape(1, n))


def solution(mesh):
    return jax.shard_map(
        functools.partial(shards, mesh.shape["row"], mesh.shape["col"]),
        mesh=mesh,
        in_specs=(P(("row", "col"), None), P(("row", "col"))),
        out_specs=P(("row", "col"), None),
        check_vma=False,
    )
```

```python
import functools

import jax
import jax.numpy as jnp
from jax import lax
from jax.experimental import pallas as pl
from jax.experimental.pallas import tpu as pltpu
from jax.sharding import PartitionSpec as P

CLUSTER_COUNT = 128
SWEEPS = 2
ANNEAL_TEMP_VALUE = 0.02
MESH = pl.DeviceIdType.MESH


def flip(index, offset, size):
    out, bit = 0, 1
    while bit < size:
        out = out + bit * ((index // bit + offset // bit) % 2)
        bit *= 2
    return out


def split3(x):
    first = x.astype(jnp.bfloat16)
    rest = x - first.astype(jnp.float32)
    second = rest.astype(jnp.bfloat16)
    third = (rest - second.astype(jnp.float32)).astype(jnp.bfloat16)
    return first, second, third


def nt(a, b):
    return lax.dot_general(
        a, b, (((1,), (1,)), ((), ())), preferred_element_type=jnp.float32
    )


def nn(a, b):
    return jnp.dot(a, b, preferred_element_type=jnp.float32)


def seeds_to_member(seeds):
    points = seeds.shape[1]
    labels = lax.broadcasted_iota(jnp.int32, (CLUSTER_COUNT, points), 0)
    chosen = jnp.where(labels == seeds, 0.5, 0.0).astype(jnp.float32)
    return chosen.T + 0.5 / CLUSTER_COUNT


def kernel(
    R, C, e_ref, s_ref, o_ref,
    e_row, e_col, s_row, s_col, c1, c2, c3, csq, d1, d2, d3, m1, m2, m3, m_row,
    m_own, m_col, pp, pin, psum, rin, az_own, az_in, acc,
    er_s, er_r, rel_s, rel_r, ec_s, ec_r, sr_s, sr_r, sc_s, sc_r,
    px_s, px_r, rs_s, rs_r, az_s, az_r,
    mz_s, mz_r, mc_s, mc_r, mrel_s, mrel_r,
):
    n = e_ref.shape[0]
    Q = C // 2
    r = lax.axis_index("row")
    c = lax.axis_index("col")
    q, b = c // 2, c % 2
    started = []

    def send(src, dst, ssem, rsem, row, col):
        copy = pltpu.make_async_remote_copy(
            src_ref=src, dst_ref=dst, send_sem=ssem, recv_sem=rsem,
            device_id=(row, col), device_id_type=MESH,
        )
        copy.start()
        started.append(copy)
        return copy

    def row_peer(t):
        return flip(r, t, R)

    def chip_peer(s):
        return flip(q, s, Q)

    def col_of(chip, core):
        return chip * 2 + core

    def block(i):
        return pl.ds(i * n, n) if isinstance(i, int) else pl.ds(pl.multiple_of(i * n, n), n)

    def column_slot(t):
        return block(arrival.index(t))

    def row_slot(s, core):
        return block(2 * s + core)

    def pair_slot(s):
        return pl.ds(2 * s * n, 2 * n)

    partner = col_of(q, 1 - b)
    group = 2 if R % 2 == 0 else 1
    near = [1 << i for i in range(R.bit_length() - 1)]
    arrival = [0] + near[::-1] + [t for t in range(1, R) if t not in near]
    groups = [arrival[g : g + group] for g in range(0, R, group)]
    row_order = arrival[1:]
    chip_order = list(range(Q - 1, 0, -1))

    def bits(size):
        return [1 << i for i in range(size.bit_length() - 1)]

    barrier = pltpu.get_barrier_semaphore()
    for t in bits(R):
        pl.semaphore_signal(barrier, inc=1, device_id=(row_peer(t), c), device_id_type=MESH)
    for u in bits(C):
        pl.semaphore_signal(barrier, inc=1, device_id=(r, flip(c, u, C)), device_id_type=MESH)

    def ready_column(x, t):
        at = column_slot(t)
        p1, p2, p3 = split3(x)
        c1[at, :] = p1
        c2[at, :] = p2
        c3[at, :] = p3
        q1, q2, q3 = split3(x * x)
        ones = jnp.ones((8, x.shape[1]), jnp.bfloat16)
        csq[:, at] = (nt(ones, q3) + nt(ones, q2)) + nt(ones, q1)

    e_row[row_slot(0, b), :] = e_ref[...]
    own_member = seeds_to_member(s_ref[...])
    m_row[row_slot(0, b), :] = own_member
    m1[block(0), :] = own_member.astype(jnp.bfloat16)
    ready_column(e_ref[...], 0)

    pl.semaphore_wait(barrier, len(bits(R)) + len(bits(C)))

    seeds_col, seeds_rw, direct, alongz = {}, {}, {}, {}

    def send_seeds_col(u):
        seeds_col[u] = send(
            s_ref, s_row.at[(u // 2) * 2 + b], sr_s.at[u], sr_r.at[u], r, flip(c, u, C)
        )

    def send_seeds_rw(t):
        seeds_rw[t] = send(s_ref, s_col.at[t], sc_s.at[t], sc_r.at[t], row_peer(t), c)

    def send_alongz(t):
        alongz[t] = send(e_ref, e_col.at[column_slot(t)], ec_s.at[t], ec_r.at[t], row_peer(t), c)

    def send_direct(s):
        direct[s] = send(
            e_ref, e_row.at[row_slot(s, b)], er_s.at[s], er_r.at[s], r,
            partner if s == 0 else col_of(chip_peer(s), b),
        )

    for t in bits(R):
        send_seeds_rw(t)
    for u in bits(C):
        send_seeds_col(u)
    far_rows, far_chips = bits(R)[::-1], bits(C)[:0:-1]
    for i in range(max(len(far_rows), len(far_chips))):
        if i < len(far_rows):
            send_alongz(far_rows[i])
        if i < len(far_chips):
            send_direct(far_chips[i] // 2)
    send_direct(0)

    heard_row, heard_col = set(), set()
    for t in range(1, R):
        if t not in bits(R):
            via = t - (1 << (t.bit_length() - 1))
            if via not in heard_row:
                seeds_rw[via].wait_recv()
                heard_row.add(via)
            send_seeds_rw(t)
            send_alongz(t)
    for u in range(1, C):
        if u not in bits(C):
            via = u - (1 << (u.bit_length() - 1))
            if via not in heard_col:
                seeds_col[via].wait_recv()
                heard_col.add(via)
            send_seeds_col(u)
            if u % 2 == 0:
                send_direct(u // 2)

    for u in range(1, C):
        if u not in heard_col:
            seeds_col[u].wait_recv()
        core = (b + u) % 2
        m_row[row_slot(u // 2, core), :] = seeds_to_member(s_row[(u // 2) * 2 + core])
    for t in range(1, R):
        if t not in heard_row:
            seeds_rw[t].wait_recv()
        m1[column_slot(t), :] = seeds_to_member(s_col[t]).astype(jnp.bfloat16)

    relay = {}
    for s in range(1, Q):
        direct[s].wait_recv()
        at = row_slot(s, b)
        relay[s] = send(e_row.at[at], e_row.at[at], rel_s.at[s], rel_r.at[s], r, partner)

    def span(ts):
        return pl.ds(arrival.index(ts[0]) * n, len(ts) * n)

    def make_distance(s, ts):
        pair, cols = pair_slot(s), span(ts)
        x = e_row[pair, :]
        x1, x2, x3 = split3(x)
        k1, k2, k3 = c1[cols, :], c2[cols, :], c3[cols, :]
        inner = nt(x3, k1) + nt(x2, k2) + nt(x1, k3)
        inner = inner + (nt(x2, k1) + nt(x1, k2))
        inner = inner + nt(x1, k1)
        sq = jnp.sum(x * x, axis=1, keepdims=True)
        distance = jnp.sqrt(sq + csq[0:1, cols] - 2.0 * inner + 1.0)
        p1, p2, p3 = split3(distance)
        d1[pair, cols] = p1
        d2[pair, cols] = p2
        d3[pair, cols] = p3
        a1 = m1[cols, :]
        return (nn(p3, a1) + nn(p2, a1)) + nn(p1, a1)

    def take_distance(s, ts):
        pair, cols = pair_slot(s), span(ts)
        p1, p2, p3 = d1[pair, cols], d2[pair, cols], d3[pair, cols]
        a1, a2, a3 = m1[cols, :], m2[cols, :], m3[cols, :]
        low = nn(p3, a1) + nn(p2, a2) + nn(p1, a3)
        return low + (nn(p2, a1) + nn(p1, a2)) + nn(p1, a1)

    log_member = None
    mz, mc, mrel = {}, {}, {}
    for w in range(SWEEPS):
        order = list(range(Q - 1, -1, -1))
        exchange, scatter = {}, {}

        def combine(s):
            exchange[s].wait_recv()
            psum[w, s] = pp[w, s, b] + pin[w, s]
            if s:
                scatter[s] = send(
                    psum.at[w, s], rin.at[w, s], rs_s.at[w, s], rs_r.at[w, s],
                    r, col_of(chip_peer(s), b),
                )

        cohesion = jnp.zeros((1, CLUSTER_COUNT), jnp.float32)
        products = make_distance if w == 0 else take_distance
        last = None
        for at, ts in enumerate(groups):
            for t in ts:
                if t == 0:
                    continue
                if w == 0:
                    alongz[t].wait_recv()
                    ready_column(e_col[column_slot(t), :], t)
                else:
                    mz[t].wait_recv()
                    ready_member(m_col[column_slot(t), :], t)
            final = at + 1 == len(groups)
            for s in (range(Q) if at == 0 else order):
                if at == 0 and w == 0:
                    (direct[0] if s == 0 else relay[s]).wait_recv()
                part = products(s, ts)
                if at:
                    part = part + acc[s]
                if not final:
                    acc[s] = part
                    continue
                pp[w, s, 0] = part[:n]
                pp[w, s, 1] = part[n:]
                exchange[s] = send(
                    pp.at[w, s, 1 - b], pin.at[w, s], px_s.at[w, s], px_r.at[w, s], r, partner
                )
                if w:
                    (mc[0] if s == 0 else mrel[s]).wait_recv()
                cohesion = cohesion + jnp.sum(
                    m_row[pair_slot(s), :] * part, axis=0, keepdims=True
                )
                if last is not None:
                    combine(last)
                last = s
            if w and at == 0:
                for s in range(1, Q):
                    mc[s].wait_recv()
                    slot = row_slot(s, b)
                    mrel[s] = send(m_row.at[slot], m_row.at[slot], mrel_s.at[s], mrel_r.at[s], r, partner)

        counts = jnp.sum(own_member, axis=0, keepdims=True)
        az_own[w, 0:1, :] = counts
        az_own[w, 1:2, :] = cohesion
        shares = {}
        for t in range(R - 1, -1, -1):
            for u in range(C - 1, -1, -1):
                if t or u:
                    i = t * C + u
                    shares[i] = send(
                        az_own.at[w], az_in.at[w, i], az_s.at[w, i], az_r.at[w, i],
                        row_peer(t), flip(c, u, C),
                    )
        combine(last)
        attraction = psum[w, 0]
        for s in order:
            if s:
                scatter[s].wait_recv()
                attraction = attraction + rin[w, s]
        for i in shares:
            shares[i].wait_recv()
        az_in[w, 0] = az_own[w]
        sums = jnp.sum(az_in[w], axis=0)
        counts, cohesion = sums[0:1, :], sums[1:2, :]
        pair_energy = attraction / counts - cohesion / (2.0 * counts * counts)
        logits = -pair_energy / ANNEAL_TEMP_VALUE
        highest = jnp.max(logits, axis=1, keepdims=True)
        total = jnp.sum(jnp.exp(logits - highest), axis=1, keepdims=True)
        log_member = logits - highest - jnp.log(total)
        if w + 1 < SWEEPS:
            own_member = jnp.exp(log_member)
            m_own[...] = own_member
            for i in range(max(R, Q) - 1):
                if i < R - 1:
                    t = row_order[i]
                    mz[t] = send(m_own, m_col.at[column_slot(t)], mz_s.at[t], mz_r.at[t], row_peer(t), c)
                if i < Q - 1:
                    s = chip_order[i]
                    mc[s] = send(
                        m_own, m_row.at[row_slot(s, b)], mc_s.at[s], mc_r.at[s],
                        r, col_of(chip_peer(s), b),
                    )
            mc[0] = send(m_own, m_row.at[row_slot(0, b)], mc_s.at[0], mc_r.at[0], r, partner)
            m_row[row_slot(0, b), :] = own_member

            def ready_member(x, t):
                at = column_slot(t)
                p1, p2, p3 = split3(x)
                m1[at, :] = p1
                m2[at, :] = p2
                m3[at, :] = p3

            ready_member(own_member, 0)

    o_ref[...] = log_member
    for copy in started:
        copy.wait_send()


def shards(R, C, embedding, seed_cluster):
    n, features = embedding.shape
    k = CLUSTER_COUNT
    Q = C // 2
    f32, bf16, i32 = jnp.float32, jnp.bfloat16, jnp.int32
    dma = pltpu.SemaphoreType.DMA
    V = pltpu.VMEM
    return pl.pallas_call(
        functools.partial(kernel, R, C),
        out_shape=jax.ShapeDtypeStruct((n, k), f32),
        in_specs=[pl.BlockSpec(memory_space=pltpu.VMEM)] * 2,
        out_specs=pl.BlockSpec(memory_space=pltpu.VMEM),
        scratch_shapes=[
            V((C * n, features), f32), V((R * n, features), f32),
            V((C, 1, n), i32), V((R, 1, n), i32),
            V((R * n, features), bf16), V((R * n, features), bf16), V((R * n, features), bf16),
            V((8, R * n), f32),
            V((C * n, R * n), bf16), V((C * n, R * n), bf16), V((C * n, R * n), bf16),
            V((R * n, k), bf16), V((R * n, k), bf16), V((R * n, k), bf16),
            V((C * n, k), f32),
            V((n, k), f32), V((R * n, k), f32),
            V((SWEEPS, Q, 2, n, k), f32), V((SWEEPS, Q, n, k), f32),
            V((SWEEPS, Q, n, k), f32), V((SWEEPS, Q, n, k), f32),
            V((SWEEPS, 2, k), f32), V((SWEEPS, R * C, 2, k), f32),
            V((Q, 2 * n, k), f32),
            dma((Q,)), dma((Q,)), dma((Q,)), dma((Q,)), dma((R,)), dma((R,)),
            dma((C,)), dma((C,)), dma((R,)), dma((R,)),
            dma((SWEEPS, Q)), dma((SWEEPS, Q)), dma((SWEEPS, Q)), dma((SWEEPS, Q)),
            dma((SWEEPS, R * C)), dma((SWEEPS, R * C)),
            dma((R,)), dma((R,)), dma((Q,)), dma((Q,)), dma((Q,)), dma((Q,)),
        ],
        compiler_params=pltpu.CompilerParams(
            collective_id=0, has_side_effects=True, vmem_limit_bytes=60 * 1024 * 1024
        ),
    )(embedding, seed_cluster.reshape(1, n))


def solution(mesh):
    return jax.shard_map(
        functools.partial(shards, mesh.shape["row"], mesh.shape["col"]),
        mesh=mesh,
        in_specs=(P(("row", "col"), None), P(("row", "col"))),
        out_specs=P(("row", "col"), None),
        check_vma=False,
    )
```
